256 devices in a mesh: ens: 4 (over z_lo, core), state: 64 (over y, z_hi, x).
Axes of the slice: x: 4, y: 4, z: 8 (z_hi: 4, z_lo: 2; z = z_hi * 2 + z_lo), core: 2. Of those that a mesh axis runs over, the one named last changes fastest.
Arguments:
- ensemble: float32 [24576, 4096], P('state', 'ens'), may hold values from -18 to 18
- obs_values: float32 [2, 256], replicated, may hold values from -6 to 6
- obs_noise: bfloat16 [2, 256, 4096], P(None, None, 'ens'), may hold values from -6 to 6
- obs_var: float32 [2, 256], replicated, may hold values from 0.25 to 2
- obs_offset: int32 [2, 256], replicated, may hold values from 0 to 383, as said below
- owner: int32 [2], replicated, may hold values from 0 to 63
Outputs:
- analysis: float32 [24576, 4096], P('state', 'ens')
The draws below stay inside these ranges and needn't reach their ends.
Inputs may be any that keep to these rules, and one draw needn't show every extreme that they name: `obs_offset`: the 256 offsets of one batch are distinct.
All inputs are finite; a program needn't handle non-finite values.
Results may differ from the reference program's by a relative error of at most 0.0003.
Values sent between devices are 32-bit elements; how exact they have to be, the bound alone decides.
No kernel may reach another device: no remote copies, remote signals or barrier semaphores. Data moves between devices by JAX's collectives and lax.ppermute only.
A program may use at most 64 MiB of HBM per device.

```python
import math
import jax
import jax.numpy as jnp
from jax import lax

S_DEV = 384
M_SUB = 1024
P_SIZE = 256
NB = 2
NS = 24576
M = 4096
LOC = 6144
N_ENS = 4
N_STATE = 64


def draw_ensemble(key, part):
    key_centre = jax.random.fold_in(key, 11)
    key_scale = jax.random.fold_in(key, 12)
    key_member = jax.random.fold_in(key, 13)
    centre = jnp.clip(jax.random.normal(key_centre, (NS, 1), jnp.float32), -3.0, 3.0)
    scale = jnp.exp(jax.random.uniform(key_scale, (NS, 1), jnp.float32, jnp.log(0.3), jnp.log(3.0)))
    member = jnp.clip(jax.random.normal(key_member, (NS, M), jnp.float32), -5.0, 5.0)
    return (centre + scale * member).astype(jnp.float32)


def draw_obs_offset(key, part):
    batch_keys = jax.random.split(jax.random.fold_in(key, 21), NB)
    return jax.vmap(lambda single: jax.random.permutation(single, S_DEV)[:P_SIZE])(batch_keys).astype(jnp.int32)


def block_levels(rng, dims, cuts, low, top_value):
    def one(dim, shards_of):
        heights = jax.random.uniform(jax.random.fold_in(jax.random.fold_in(rng, 6), dim), (shards_of,), jnp.float32, low / len(cuts), top_value / len(cuts))
        return jnp.repeat(jnp.exp(heights), dims[dim] // shards_of).reshape((-1,) + (1,) * (len(dims) - dim - 1))

    level = one(*cuts[0])
    for cut in cuts[1:]:
        level = level * one(*cut)
    return level


def normal_values(key, dims, scale, most, cuts=(), held_as=jnp.bfloat16):
    array = scale * jax.random.normal(key, dims, jnp.float32)
    if cuts:
        array = array * block_levels(key, dims, cuts, -0.22, 0.18)
    return jnp.clip(array, -most, most).astype(held_as)


def setup_inputs(seed: int = 0) -> dict:
    streams_of = jax.random.split(jax.random.key(seed), 7)
    return {
        "ensemble": draw_ensemble(jax.random.fold_in(streams_of[6], 71), 0),
        "obs_values": normal_values(streams_of[1], (NB, P_SIZE), 1.0, 6.0, (), jnp.float32),
        "obs_noise": normal_values(streams_of[2], (NB, P_SIZE, M), 1.0, 6.0, ((2, 4),)),
        "obs_var": jnp.clip(jnp.exp(jax.random.uniform(streams_of[3], (NB, P_SIZE), jnp.float32, math.log(0.25), math.log(2.0))), 0.25, 2.0),
        "obs_offset": draw_obs_offset(jax.random.fold_in(streams_of[6], 71), 0),
        "owner": jax.random.randint(streams_of[5], (NB,), 0, N_STATE).astype(jnp.int32),
    }


finest = lax.Precision.HIGHEST

def cycle_taper(first, second, total, reach):
    distance = jnp.abs(first - second)
    distance = jnp.minimum(distance, total - distance).astype(jnp.float32)
    ratio = distance / jnp.float32(reach)
    return 1.0 / (1.0 + ratio * ratio)

def reference(ensemble, obs_values, obs_noise, obs_var, obs_offset, owner):
    states = S_DEV * N_STATE
    members = M_SUB * N_ENS
    current = ensemble
    for batch in range(NB):
        places = (owner[batch] * S_DEV + obs_offset[batch]).astype(jnp.int32)
        prior = current[places]
        obs_anom = prior - (lax.optimization_barrier(jnp.sum(prior, axis=1)) / members)[:, None]
        spread = jnp.einsum('pm,qm->pq', obs_anom, obs_anom, precision=finest)
        obs_cov = cycle_taper(places[:, None], places[None, :], states, LOC) * (spread / (members - 1)) + jnp.diag(obs_var[batch])
        factor = jnp.linalg.cholesky(obs_cov)
        variance = obs_var[batch]
        misfit = obs_values[batch][:, None] + jnp.sqrt(variance)[:, None] * obs_noise[batch].astype(jnp.float32) - prior
        solved = jax.scipy.linalg.cho_solve((factor, True), misfit)
        blocks = current.reshape(N_STATE, S_DEV, members)
        block_ids = jnp.arange(N_STATE, dtype=jnp.int32)

        def update(item_pair):
            block, block_id = item_pair
            positions = block_id * S_DEV + jnp.arange(S_DEV, dtype=jnp.int32)
            cross = jnp.einsum('sm,pm->sp', block, obs_anom, precision=finest)
            gain = cycle_taper(positions[:, None], places[None, :], states, LOC) * (cross / (members - 1))
            return block + jnp.dot(gain.astype(jnp.float32), solved.astype(jnp.float32), precision=finest, preferred_element_type=jnp.float32)
        current = lax.map(update, (blocks, block_ids)).reshape(states, members)
    return current
```

```python
import jax
import jax.numpy as jnp
from jax import lax
from jax.experimental import pallas as pl
from jax.experimental.pallas import tpu as pltpu
from jax.sharding import Mesh, PartitionSpec as P

NB = 2
finest = lax.Precision.HIGHEST
ENS = ("zl", "core")
PLANE = ("y", "x")
STATE = ("y", "zh", "x")
GROUP = 8
LANES = 128


def cycle_taper(first, second, total, reach):
    distance = jnp.abs(first - second)
    distance = jnp.minimum(distance, total - distance).astype(jnp.float32)
    ratio = distance / jnp.float32(reach)
    return 1.0 / (1.0 + ratio * ratio)


def swap(value, axis):
    return lax.ppermute(value, axis, [(0, 1), (1, 0)])


def ens_sum(value):
    half = value.shape[0] // 2
    first = lax.axis_index("core") == 0
    top, bottom = value[:half], value[half:]
    kept = jnp.where(first, top, bottom) + swap(jnp.where(first, bottom, top), "core")
    kept = kept + swap(kept, "zl")
    other = swap(kept, "core")
    return jnp.concatenate(
        [jnp.where(first, kept, other), jnp.where(first, other, kept)], axis=0
    )


def plane_exchange(rows):
    planes = lax.axis_size(PLANE)
    blocks = rows.reshape(planes, rows.shape[0] // planes, rows.shape[1])
    return lax.all_to_all(blocks, PLANE, 0, 0)


def spread_rows(current, offsets, owner):
    ny, nz, nx = (lax.axis_size(a) for a in STATE)
    here = lax.axis_index(STATE)
    oy, oz, ox = owner // (nz * nx), (owner // nx) % nz, owner % nx
    source = oy * nx + ox
    chosen = jnp.where(here == owner[0], offsets[0], offsets[1])
    received = plane_exchange(jnp.take(current, chosen, axis=0))
    first = lax.dynamic_index_in_dim(received, source[0], 0, False)

    def again(_):
        extra = plane_exchange(jnp.take(current, offsets[1], axis=0))
        return lax.dynamic_index_in_dim(extra, source[1], 0, False)

    def same(kept):
        return lax.dynamic_index_in_dim(kept, source[1], 0, False)

    second = lax.cond(owner[0] == owner[1], again, same, received)
    pair = jnp.stack([first, second])
    mine = lax.axis_index("zh")
    best = pair
    for shift in (1, nz - 1, 2):
        moved = lax.ppermute(pair, "zh", [(i, (i + shift) % nz) for i in range(nz)])
        best = jnp.where(((mine - shift) % nz == oz)[:, None, None], moved, best)
    planes = ny * nx
    out = []
    for batch in range(NB):
        whole = jnp.broadcast_to(best[batch][None], (planes,) + best[batch].shape)
        out.append(lax.all_to_all(whole, PLANE, 0, 0).reshape(-1, current.shape[1]))
    return out


def inverse_kernel(members, states, reach, spread, var_row, off_col, off_row, out):
    size = spread.shape[0]
    tiles = size // LANES
    rows = lax.broadcasted_iota(jnp.int32, (size, LANES), 0)
    lanes = lax.broadcasted_iota(jnp.int32, (size, LANES), 1)
    for t in range(tiles):
        cols = slice(t * LANES, (t + 1) * LANES)
        cov = cycle_taper(off_col[...], off_row[:, cols], states, reach) * (
            spread[:, cols] / (members - 1)
        )
        out[t] = cov + jnp.where(rows == lanes + t * LANES, var_row[:, cols], 0.0)
    row8 = lax.broadcasted_iota(jnp.int32, (GROUP, LANES), 0)
    lane8 = lax.broadcasted_iota(jnp.int32, (GROUP, LANES), 1)

    def tile_step(t, carry):
        for s in range(LANES // GROUP):
            base = s * GROUP
            at = pl.multiple_of(t * LANES + base, GROUP)
            block = out[t, pl.ds(at, GROUP), :]
            cols = [
                jnp.broadcast_to(block[:, base + j : base + j + 1], (GROUP, LANES))
                for j in range(GROUP)
            ]
            inside = (lane8 >= base) & (lane8 < base + GROUP)
            unit = (lane8 - base == row8).astype(jnp.float32)
            pivot_rows = []
            for q in range(tiles):
                piece = out[q, pl.ds(at, GROUP), :]
                pivot_rows.append(jnp.where(inside & (q == t), unit, piece))
            for k in range(GROUP):
                inv = 1.0 / jnp.broadcast_to(cols[k][k : k + 1], (GROUP, LANES))
                factor = cols[k]
                on_row = row8 == k

                def eliminate(x):
                    scaled = jnp.broadcast_to(x[k : k + 1], (GROUP, LANES)) * inv
                    return jnp.where(on_row, scaled, x - factor * scaled)

                for j in range(k + 1, GROUP):
                    cols[j] = eliminate(cols[j])
                pivot_rows = [eliminate(x) for x in pivot_rows]
            spreads = [
                [jnp.broadcast_to(x[j : j + 1], (GROUP, LANES)) for j in range(GROUP)]
                for x in pivot_rows
            ]
            for g in range(size // GROUP):
                place = slice(g * GROUP, (g + 1) * GROUP)
                panel = out[t, place, :]
                factors = [
                    jnp.broadcast_to(panel[:, base + j : base + j + 1], (GROUP, LANES))
                    for j in range(GROUP)
                ]
                for q in range(tiles):
                    acc = jnp.where(inside & (q == t), 0.0, out[q, place, :])
                    for j in range(GROUP):
                        acc = acc - factors[j] * spreads[q][j]
                    out[q, place, :] = acc
            for q in range(tiles):
                out[q, pl.ds(at, GROUP), :] = pivot_rows[q]
        return carry

    lax.fori_loop(0, tiles, tile_step, 0)


def inverse_cov(spread, variance, places, members, states, reach):
    size = spread.shape[0]

    def body(*refs):
        inverse_kernel(members, states, reach, *refs)

    tiled = pl.pallas_call(
        body,
        out_shape=jax.ShapeDtypeStruct((size // LANES, size, LANES), jnp.float32),
        compiler_params=pltpu.CompilerParams(vmem_limit_bytes=16 << 20),
    )(spread, variance[None, :], places[:, None], places[None, :])
    return jnp.concatenate([tiled[t] for t in range(size // LANES)], axis=1)


def local(ensemble, obs_values, obs_noise, obs_var, obs_offset, owner):
    rows, width = ensemble.shape
    members = width * lax.axis_size(ENS)
    states = rows * lax.axis_size(STATE)
    reach = states // 4
    here = lax.axis_index(STATE)
    positions = here * rows + jnp.arange(rows, dtype=jnp.int32)
    places = [owner[b] * rows + obs_offset[b] for b in range(NB)]
    priors = spread_rows(ensemble, obs_offset, owner)
    current = jnp.concatenate([ensemble, priors[1]], axis=0)
    where = jnp.concatenate([positions, places[1]], axis=0)
    prior = priors[0]
    for batch in range(NB):
        mean = lax.psum(jnp.sum(prior, axis=1), ENS) / members
        anom = prior - mean[:, None]
        spread = ens_sum(jnp.einsum("pm,qm->pq", anom, anom, precision=finest))
        cross = ens_sum(jnp.einsum("sm,pm->sp", current, anom, precision=finest))
        inverse = inverse_cov(spread, obs_var[batch], places[batch], members, states, reach)
        gain = cycle_taper(where[:, None], places[batch][None, :], states, reach) * (
            cross / (members - 1)
        )
        gain = jnp.dot(gain, inverse, precision=finest)
        misfit = (
            obs_values[batch][:, None]
            + jnp.sqrt(obs_var[batch])[:, None] * obs_noise[batch].astype(jnp.float32)
            - prior
        )
        current = current + jnp.dot(gain, misfit, precision=finest)
        prior = current[rows:]
        current = current[:rows]
        where = positions
    return current


def solution(mesh):
    ens, state = mesh.devices.shape
    fine = Mesh(
        mesh.devices.reshape(2, ens // 2, 4, state // 16, 4), ("zl", "core", "y", "zh", "x")
    )
    in_specs = (P(STATE, ENS), P(), P(None, None, ENS), P(), P(), P())
    return jax.shard_map(
        local, mesh=fine, in_specs=in_specs, out_specs=P(STATE, ENS), check_vma=False
    )
```

```python
import jax
import jax.numpy as jnp
from jax import lax
from jax.experimental import pallas as pl
from jax.experimental.pallas import tpu as pltpu
from jax.sharding import Mesh, PartitionSpec as P

NB = 2
finest = lax.Precision.HIGHEST
close = lax.Precision.HIGH
ENS = ("zl", "core")
PLANE = ("y", "x")
STATE = ("y", "zh", "x")
GROUP = 8
STEP = 16
LANES = 128


def cycle_taper(first, second, total, reach):
    distance = jnp.abs(first - second)
    distance = jnp.minimum(distance, total - distance).astype(jnp.float32)
    ratio = distance / jnp.float32(reach)
    return 1.0 / (1.0 + ratio * ratio)


def swap(value, axis):
    return lax.ppermute(value, axis, [(0, 1), (1, 0)])


def ens_sum(value):
    half = value.shape[0] // 2
    first = lax.axis_index("core") == 0
    top, bottom = value[:half], value[half:]
    kept = jnp.where(first, top, bottom) + swap(jnp.where(first, bottom, top), "core")
    kept = kept + swap(kept, "zl")
    other = swap(kept, "core")
    return jnp.concatenate(
        [jnp.where(first, kept, other), jnp.where(first, other, kept)], axis=0
    )


def plane_exchange(rows):
    planes = lax.axis_size(PLANE)
    blocks = rows.reshape(planes, rows.shape[0] // planes, rows.shape[1])
    return lax.all_to_all(blocks, PLANE, 0, 0)


def pick_rows(current, offsets):
    return current.at[offsets].get(mode="promise_in_bounds", unique_indices=True)


def along_z(part, source):
    size = lax.axis_size("zh")
    mine = lax.axis_index("zh")
    best = part
    for shift in (1, size - 1, 2):
        moved = lax.ppermute(part, "zh", [(i, (i + shift) % size) for i in range(size)])
        best = jnp.where((mine - shift) % size == source, moved, best)
    return best


def plane_gather(part):
    planes = lax.axis_size(PLANE)
    whole = jnp.broadcast_to(part[None], (planes,) + part.shape)
    return lax.all_to_all(whole, PLANE, 0, 0).reshape(-1, part.shape[1])


def spread_rows(current, offsets, owner):
    ny, nz, nx = (lax.axis_size(a) for a in STATE)
    here = lax.axis_index(STATE)
    oz = (owner // nx) % nz
    source = owner // (nz * nx) * nx + owner % nx
    chosen = jnp.where(here == owner[0], offsets[0], offsets[1])
    received = plane_exchange(pick_rows(current, chosen))
    first = lax.dynamic_index_in_dim(received, source[0], 0, False)
    second = lax.dynamic_index_in_dim(received, source[1], 0, False)
    first = along_z(first, oz[0])
    first, second = lax.optimization_barrier((first, second))
    prior = plane_gather(first)

    def again(_):
        extra = plane_exchange(pick_rows(current, offsets[1]))
        return lax.dynamic_index_in_dim(extra, source[1], 0, False)

    second = lax.cond(owner[0] == owner[1], again, lambda kept: kept, second)
    return prior, plane_gather(along_z(second, oz[1]))


def moments_kernel(prior, out):
    size, width = prior.shape
    half = size // 2
    value = prior[...]
    anom = value - jnp.sum(value, axis=1, keepdims=True) / width
    blocks = ((0, 0), (1, 0), (1, 1))
    for n, (i, j) in enumerate(blocks):
        out[n * half : (n + 1) * half, :] = lax.dot_general(
            anom[i * half : (i + 1) * half],
            anom[j * half : (j + 1) * half],
            (((1,), (1,)), ((), ())),
            precision=finest,
            preferred_element_type=jnp.float32,
        )
    mean = lax.dot_general(
        jnp.ones((GROUP, width), jnp.float32),
        value,
        (((1,), (1,)), ((), ())),
        precision=finest,
        preferred_element_type=jnp.float32,
    ) / width
    row = lax.broadcasted_iota(jnp.int32, (GROUP, half), 0)
    out[3 * half :, :] = jnp.where(
        row == 0, mean[:, :half], jnp.where(row == 1, mean[:, half:], 0.0)
    )


def moments(prior):
    size = prior.shape[0]
    return pl.pallas_call(
        moments_kernel,
        out_shape=jax.ShapeDtypeStruct((3 * size // 2 + GROUP, size // 2), jnp.float32),
        compiler_params=pltpu.CompilerParams(vmem_limit_bytes=24 << 20),
        cost_estimate=pl.CostEstimate(
            flops=6 * size * size * prior.shape[1] * 2,
            bytes_accessed=4 * size * prior.shape[1],
            transcendentals=0,
        ),
    )(prior)


def merged(mine, other, count):
    half = mine.shape[1]
    delta = mine[3 * half :] - other[3 * half :]
    row = lax.broadcasted_iota(jnp.int32, delta.shape, 0)
    parts = [jnp.where(row == 0, jnp.broadcast_to(delta[i : i + 1], delta.shape), 0.0) for i in (0, 1)]
    out = []
    for n, (i, j) in enumerate(((0, 0), (1, 0), (1, 1))):
        place = slice(n * half, (n + 1) * half)
        outer = lax.dot_general(
            parts[i],
            parts[j],
            (((0,), (0,)), ((), ())),
            precision=finest,
            preferred_element_type=jnp.float32,
        )
        out.append(mine[place] + other[place] + outer * (count / 2))
    out.append((mine[3 * half :] + other[3 * half :]) / 2)
    return out


def merge_kernel(count, mine, other, out):
    half = mine.shape[1]
    parts = merged(mine[...], other[...], count)
    for n in range(3):
        out[n * half : (n + 1) * half, :] = parts[n]
    out[3 * half :, :] = parts[3]


def merge(mine, other, count):
    def body(*refs):
        merge_kernel(count, *refs)

    return pl.pallas_call(
        body,
        out_shape=jax.ShapeDtypeStruct(mine.shape, jnp.float32),
        compiler_params=pltpu.CompilerParams(vmem_limit_bytes=16 << 20),
    )(mine, other)


def inverse_kernel(members, states, reach, mine, other, var_row, off_col, off_row, out):
    half = LANES
    size = 2 * half
    tiles = 2
    parts = merged(mine[...], other[...], members // 2)
    square = ((parts[0], parts[1]), (parts[1].T, parts[2]))
    rows = lax.broadcasted_iota(jnp.int32, (half, half), 0)
    lanes = lax.broadcasted_iota(jnp.int32, (half, half), 1)
    for t in range(tiles):
        cols = slice(t * half, (t + 1) * half)
        for i in range(tiles):
            place = slice(i * half, (i + 1) * half)
            cov = cycle_taper(off_col[place], off_row[:, cols], states, reach) * (
                square[t][i] / (members - 1)
            )
            if i == t:
                cov = cov + jnp.where(rows == lanes, var_row[:, cols], 0.0)
            out[t, place, :] = cov
    row = lax.broadcasted_iota(jnp.int32, (STEP, half), 0)
    lane = lax.broadcasted_iota(jnp.int32, (STEP, half), 1)
    wide = lax.broadcasted_iota(jnp.int32, (size, half), 1)

    def over(x):
        return jnp.broadcast_to(x, (STEP, half))

    current = [out[q, 0:STEP, :] for q in range(tiles)]
    for at in range(0, size, STEP):
        t, base = divmod(at, half)
        inside = (lane >= base) & (lane < base + STEP)
        unit = (lane - base == row).astype(jnp.float32)
        columns = [over(current[t][:, base + j : base + j + 1]) for j in range(STEP)]
        pivots = [jnp.where(inside, unit, x) if q == t else x for q, x in enumerate(current)]
        last = at + STEP == size
        if not last:
            ahead = [out[q, at + STEP : at + 2 * STEP, :] for q in range(tiles)]
            factors = [over(ahead[t][:, base + j : base + j + 1]) for j in range(STEP)]
        for k in range(STEP):
            inv = 1.0 / over(columns[k][k : k + 1])
            factor = columns[k]
            on_row = row == k

            def eliminate(x):
                scaled = over(x[k : k + 1]) * inv
                return jnp.where(on_row, scaled, x - factor * scaled)

            for j in range(k + 1, STEP):
                columns[j] = eliminate(columns[j])
            pivots = [eliminate(x) for x in pivots]
        if not last:
            current = []
            for q in range(tiles):
                acc = jnp.where(inside, 0.0, ahead[q]) if q == t else ahead[q]
                for j in range(STEP):
                    acc = acc - factors[j] * over(pivots[q][j : j + 1])
                current.append(acc)
        panel = out[t, :, :][:, base : base + STEP]
        for q in range(tiles):
            old = out[q]
            if q == t:
                old = jnp.where((wide >= base) & (wide < base + STEP), 0.0, old)
            out[q] = old - jnp.dot(
                panel, pivots[q], precision=finest, preferred_element_type=jnp.float32
            )
        for q in range(tiles):
            out[q, at : at + STEP, :] = pivots[q]


def inverse_cov(mine, other, variance, places, members, states, reach):
    size = places.shape[0]

    def body(*refs):
        inverse_kernel(members, states, reach, *refs)

    tiled = pl.pallas_call(
        body,
        out_shape=jax.ShapeDtypeStruct((size // LANES, size, LANES), jnp.float32),
        compiler_params=pltpu.CompilerParams(vmem_limit_bytes=16 << 20),
        cost_estimate=pl.CostEstimate(flops=8 * 10**9, bytes_accessed=1 << 20, transcendentals=0),
    )(mine, other, variance[None, :], places[:, None], places[None, :])
    return jnp.concatenate([tiled[t] for t in range(size // LANES)], axis=1)


def local(ensemble, obs_values, obs_noise, obs_var, obs_offset, owner):
    rows, width = ensemble.shape
    members = width * lax.axis_size(ENS)
    states = rows * lax.axis_size(STATE)
    reach = states // 4
    here = lax.axis_index(STATE)
    positions = here * rows + jnp.arange(rows, dtype=jnp.int32)
    places = [owner[b] * rows + obs_offset[b] for b in range(NB)]
    prior, later = spread_rows(ensemble, obs_offset, owner)
    current = [ensemble, later]
    where = [positions, places[1]]
    for batch in range(NB):
        stats = moments(prior)
        stats = merge(stats, swap(stats, "core"), width)
        other = swap(stats, "zl")
        size = prior.shape[0]
        mean = ((stats[-GROUP:] + other[-GROUP:]) / 2)[:2].reshape(size)
        anom = prior - mean[:, None]
        if batch == 0:
            anom, current[1] = lax.optimization_barrier((anom, current[1]))
        cross = ens_sum(
            jnp.concatenate(
                [jnp.einsum("sm,pm->sp", x, anom, precision=close) for x in current], axis=0
            )
        )
        inverse = inverse_cov(stats, other, obs_var[batch], places[batch], members, states, reach)
        spots = jnp.concatenate(where, axis=0)
        gain = cycle_taper(spots[:, None], places[batch][None, :], states, reach) * (
            cross / (members - 1)
        )
        gain = jnp.dot(gain, inverse, precision=close)
        misfit = (
            obs_values[batch][:, None]
            + jnp.sqrt(obs_var[batch])[:, None] * obs_noise[batch].astype(jnp.float32)
            - prior
        )
        begin = 0
        after = []
        for x in current:
            after.append(x + jnp.dot(gain[begin : begin + x.shape[0]], misfit, precision=close))
            begin += x.shape[0]
        prior = after[-1]
        current = after[:1]
        where = [positions]
    return current[0]


def solution(mesh):
    ens, state = mesh.devices.shape
    fine = Mesh(
        mesh.devices.reshape(2, ens // 2, 4, state // 16, 4), ("zl", "core", "y", "zh", "x")
    )
    in_specs = (P(STATE, ENS), P(), P(None, None, ENS), P(), P(), P())
    return jax.shard_map(
        local, mesh=fine, in_specs=in_specs, out_specs=P(STATE, ENS), check_vma=False
    )
```

```python
import jax
import jax.numpy as jnp
from jax import lax
from jax.experimental import pallas as pl
from jax.experimental.pallas import tpu as pltpu
from jax.sharding import Mesh, PartitionSpec as P

NB = 2
finest = lax.Precision.HIGHEST
close = lax.Precision.HIGH
ENS = ("zl", "core")
PLANE = ("y", "x")
STATE = ("y", "zh", "x")
GROUP = 8
STEP = 16
LANES = 128


def cycle_taper(first, second, total, reach):
    distance = jnp.abs(first - second)
    distance = jnp.minimum(distance, total - distance).astype(jnp.float32)
    ratio = distance / jnp.float32(reach)
    return 1.0 / (1.0 + ratio * ratio)


def swap(value, axis):
    return lax.ppermute(value, axis, [(0, 1), (1, 0)])


def pair_sum(value):
    half = value.shape[0] // 2
    first = lax.axis_index("core") == 0
    top, bottom = value[:half], value[half:]
    return jnp.where(first, top, bottom) + swap(jnp.where(first, bottom, top), "core")


def whole_sum(kept, moved):
    first = lax.axis_index("core") == 0
    kept = kept + moved
    other = swap(kept, "core")
    return jnp.concatenate(
        [jnp.where(first, kept, other), jnp.where(first, other, kept)], axis=0
    )


def plane_exchange(rows):
    planes = lax.axis_size(PLANE)
    blocks = rows.reshape(planes, rows.shape[0] // planes, rows.shape[1])
    return lax.all_to_all(blocks, PLANE, 0, 0)


def pick_rows(current, offsets):
    rows = lax.broadcasted_iota(jnp.int32, (offsets.shape[0], current.shape[0]), 1)
    chosen = (rows == offsets[:, None]).astype(jnp.float32)
    return jnp.dot(chosen, current, precision=finest)


def along_z(pair, source):
    size = lax.axis_size("zh")
    mine = lax.axis_index("zh")
    best = pair
    for shift in (1, size - 1, 2):
        moved = lax.ppermute(pair, "zh", [(i, (i + shift) % size) for i in range(size)])
        best = jnp.where(((mine - shift) % size == source)[:, None, None], moved, best)
    return best


def spread_rows(current, offsets, owner):
    ny, nz, nx = (lax.axis_size(a) for a in STATE)
    here = lax.axis_index(STATE)
    oz = (owner // nx) % nz
    source = owner // (nz * nx) * nx + owner % nx
    chosen = jnp.where(here == owner[0], offsets[0], offsets[1])
    received = plane_exchange(pick_rows(current, chosen))
    first = lax.dynamic_index_in_dim(received, source[0], 0, False)
    second = lax.dynamic_index_in_dim(received, source[1], 0, False)

    def again(_):
        extra = plane_exchange(pick_rows(current, offsets[1]))
        return lax.dynamic_index_in_dim(extra, source[1], 0, False)

    second = lax.cond(owner[0] == owner[1], again, lambda kept: kept, second)
    pair = along_z(jnp.stack([first, second]), oz)
    planes = ny * nx
    whole = jnp.broadcast_to(pair[:, None], (NB, planes) + pair.shape[1:])
    whole = lax.all_to_all(whole, PLANE, 1, 1)
    return whole.reshape(NB, -1, current.shape[1])


def moments_kernel(prior, out, anom_out):
    size, width = prior.shape
    half = size // 2
    value = prior[...]
    anom = value - jnp.sum(value, axis=1, keepdims=True) / width
    anom_out[...] = anom
    for n, (i, j) in enumerate(((0, 0), (1, 0), (1, 1))):
        out[n * half : (n + 1) * half, :] = lax.dot_general(
            anom[i * half : (i + 1) * half],
            anom[j * half : (j + 1) * half],
            (((1,), (1,)), ((), ())),
            precision=finest,
            preferred_element_type=jnp.float32,
        )
    mean = lax.dot_general(
        jnp.ones((GROUP, width), jnp.float32),
        value,
        (((1,), (1,)), ((), ())),
        precision=finest,
        preferred_element_type=jnp.float32,
    ) / width
    row = lax.broadcasted_iota(jnp.int32, (GROUP, half), 0)
    out[3 * half :, :] = jnp.where(
        row == 0, mean[:, :half], jnp.where(row == 1, mean[:, half:], 0.0)
    )


def moments(prior):
    size = prior.shape[0]
    return pl.pallas_call(
        moments_kernel,
        out_shape=(
            jax.ShapeDtypeStruct((3 * size // 2 + GROUP, size // 2), jnp.float32),
            jax.ShapeDtypeStruct(prior.shape, jnp.float32),
        ),
        compiler_params=pltpu.CompilerParams(vmem_limit_bytes=24 << 20),
        cost_estimate=pl.CostEstimate(
            flops=6 * size * size * prior.shape[1] * 2,
            bytes_accessed=4 * size * prior.shape[1],
            transcendentals=0,
        ),
    )(prior)


def merged(mine, other, count):
    half = mine.shape[1]
    delta = mine[3 * half :] - other[3 * half :]
    row = lax.broadcasted_iota(jnp.int32, delta.shape, 0)
    parts = [jnp.where(row == 0, jnp.broadcast_to(delta[i : i + 1], delta.shape), 0.0) for i in (0, 1)]
    out = []
    for n, (i, j) in enumerate(((0, 0), (1, 0), (1, 1))):
        place = slice(n * half, (n + 1) * half)
        outer = lax.dot_general(
            parts[i],
            parts[j],
            (((0,), (0,)), ((), ())),
            precision=finest,
            preferred_element_type=jnp.float32,
        )
        out.append(mine[place] + other[place] + outer * (count / 2))
    out.append((mine[3 * half :] + other[3 * half :]) / 2)
    return out


def merge_kernel(count, mine, other, out):
    half = mine.shape[1]
    parts = merged(mine[...], other[...], count)
    for n in range(3):
        out[n * half : (n + 1) * half, :] = parts[n]
    out[3 * half :, :] = parts[3]


def merge(mine, other, count):
    def body(*refs):
        merge_kernel(count, *refs)

    return pl.pallas_call(
        body,
        out_shape=jax.ShapeDtypeStruct(mine.shape, jnp.float32),
        compiler_params=pltpu.CompilerParams(vmem_limit_bytes=16 << 20),
    )(mine, other)


def inverse_kernel(members, states, reach, mine, other, var_row, off_col, off_row, out):
    half = LANES
    size = 2 * half
    tiles = 2
    parts = merged(mine[...], other[...], members // 2)
    square = ((parts[0], parts[1]), (parts[1].T, parts[2]))
    rows = lax.broadcasted_iota(jnp.int32, (half, half), 0)
    lanes = lax.broadcasted_iota(jnp.int32, (half, half), 1)
    for t in range(tiles):
        cols = slice(t * half, (t + 1) * half)
        for i in range(tiles):
            place = slice(i * half, (i + 1) * half)
            cov = cycle_taper(off_col[place], off_row[:, cols], states, reach) * (
                square[t][i] / (members - 1)
            )
            if i == t:
                cov = cov + jnp.where(rows == lanes, var_row[:, cols], 0.0)
            out[t, place, :] = cov
    row = lax.broadcasted_iota(jnp.int32, (STEP, half), 0)
    lane = lax.broadcasted_iota(jnp.int32, (STEP, half), 1)
    wide = lax.broadcasted_iota(jnp.int32, (size, half), 1)

    def over(x):
        return jnp.broadcast_to(x, (STEP, half))

    current = [out[q, 0:STEP, :] for q in range(tiles)]
    for at in range(0, size, STEP):
        t, base = divmod(at, half)
        inside = (lane >= base) & (lane < base + STEP)
        unit = (lane - base == row).astype(jnp.float32)
        columns = [over(current[t][:, base + j : base + j + 1]) for j in range(STEP)]
        pivots = [jnp.where(inside, unit, x) if q == t else x for q, x in enumerate(current)]
        last = at + STEP == size
        if not last:
            ahead = [out[q, at + STEP : at + 2 * STEP, :] for q in range(tiles)]
            factors = [over(ahead[t][:, base + j : base + j + 1]) for j in range(STEP)]
        for k in range(STEP):
            inv = 1.0 / over(columns[k][k : k + 1])
            factor = columns[k]
            on_row = row == k

            def eliminate(x):
                scaled = over(x[k : k + 1]) * inv
                return jnp.where(on_row, scaled, x - factor * scaled)

            for j in range(k + 1, STEP):
                columns[j] = eliminate(columns[j])
            pivots = [eliminate(x) for x in pivots]
        if not last:
            current = []
            for q in range(tiles):
                acc = jnp.where(inside, 0.0, ahead[q]) if q == t else ahead[q]
                for j in range(STEP):
                    acc = acc - factors[j] * over(pivots[q][j : j + 1])
                current.append(acc)
        panel = out[t, :, :][:, base : base + STEP]
        for q in range(tiles):
            old = out[q]
            if q == t:
                old = jnp.where((wide >= base) & (wide < base + STEP), 0.0, old)
            out[q] = old - jnp.dot(
                panel, pivots[q], precision=finest, preferred_element_type=jnp.float32
            )
        for q in range(tiles):
            out[q, at : at + STEP, :] = pivots[q]


def inverse_cov(mine, other, variance, places, members, states, reach):
    size = places.shape[0]

    def body(*refs):
        inverse_kernel(members, states, reach, *refs)

    tiled = pl.pallas_call(
        body,
        out_shape=jax.ShapeDtypeStruct((size // LANES, size, LANES), jnp.float32),
        compiler_params=pltpu.CompilerParams(vmem_limit_bytes=16 << 20),
        cost_estimate=pl.CostEstimate(flops=8 * 10**9, bytes_accessed=1 << 20, transcendentals=0),
    )(mine, other, variance[None, :], places[:, None], places[None, :])
    return jnp.concatenate([tiled[t] for t in range(size // LANES)], axis=1)


def local(ensemble, obs_values, obs_noise, obs_var, obs_offset, owner):
    rows, width = ensemble.shape
    members = width * lax.axis_size(ENS)
    states = rows * lax.axis_size(STATE)
    reach = states // 4
    here = lax.axis_index(STATE)
    positions = here * rows + jnp.arange(rows, dtype=jnp.int32)
    places = [owner[b] * rows + obs_offset[b] for b in range(NB)]
    priors = spread_rows(ensemble, obs_offset, owner)
    prior = priors[0]
    current = [ensemble, priors[1]]
    where = [positions, places[1]]
    for batch in range(NB):
        size = prior.shape[0]
        stats, anom = moments(prior)
        own_mean = stats[-GROUP:][:2]
        stats = merge(stats, swap(stats, "core"), width)
        other = swap(stats, "zl")
        cross = jnp.concatenate(
            [jnp.einsum("sm,pm->sp", x, anom, precision=close) for x in current], axis=0
        )
        total = jnp.concatenate([jnp.sum(x, axis=1) for x in current], axis=0)
        shift = own_mean - ((stats[-GROUP:] + other[-GROUP:]) / 2)[:2]
        kept = pair_sum(cross + total[:, None] * shift.reshape(1, size))
        moved = swap(kept, "zl")
        inverse = inverse_cov(stats, other, obs_var[batch], places[batch], members, states, reach)
        moved, inverse = lax.optimization_barrier((moved, inverse))
        cross = whole_sum(kept, moved)
        spots = jnp.concatenate(where, axis=0)
        gain = cycle_taper(spots[:, None], places[batch][None, :], states, reach) * (
            cross / (members - 1)
        )
        gain = jnp.dot(gain, inverse, precision=close)
        misfit = (
            obs_values[batch][:, None]
            + jnp.sqrt(obs_var[batch])[:, None] * obs_noise[batch].astype(jnp.float32)
            - prior
        )
        begin = 0
        after = []
        for x in current:
            after.append(x + jnp.dot(gain[begin : begin + x.shape[0]], misfit, precision=close))
            begin += x.shape[0]
        prior = after[-1]
        current = after[:1]
        where = [positions]
    return current[0]


def solution(mesh):
    ens, state = mesh.devices.shape
    fine = Mesh(
        mesh.devices.reshape(2, ens // 2, 4, state // 16, 4), ("zl", "core", "y", "zh", "x")
    )
    in_specs = (P(STATE, ENS), P(), P(None, None, ENS), P(), P(), P())
    return jax.shard_map(
        local, mesh=fine, in_specs=in_specs, out_specs=P(STATE, ENS), check_vma=False
    )
```

```python
import jax
import jax.numpy as jnp
from jax import lax
from jax.experimental import pallas as pl
from jax.experimental.pallas import tpu as pltpu
from jax.sharding import Mesh, PartitionSpec as P

NB = 2
finest = lax.Precision.HIGHEST
close = lax.Precision.HIGH
ENS = ("zl", "core")
PLANE = ("y", "x")
STATE = ("y", "zh", "x")
GROUP = 8
STEP = 16
LANES = 128


def cycle_taper(first, second, total, reach):
    distance = jnp.abs(first - second)
    distance = jnp.minimum(distance, total - distance).astype(jnp.float32)
    ratio = distance / jnp.float32(reach)
    return 1.0 / (1.0 + ratio * ratio)


def swap(value, axis):
    return lax.ppermute(value, axis, [(0, 1), (1, 0)])


def pair_sum(value):
    half = value.shape[0] // 2
    first = lax.axis_index("core") == 0
    top, bottom = value[:half], value[half:]
    return jnp.where(first, top, bottom) + swap(jnp.where(first, bottom, top), "core")


def whole_sum(kept, moved):
    first = lax.axis_index("core") == 0
    kept = kept + moved
    other = swap(kept, "core")
    return jnp.concatenate(
        [jnp.where(first, kept, other), jnp.where(first, other, kept)], axis=0
    )


def plane_exchange(rows):
    planes = lax.axis_size(PLANE)
    blocks = rows.reshape(planes, rows.shape[0] // planes, rows.shape[1])
    return lax.all_to_all(blocks, PLANE, 0, 0)


def pick_rows(current, offsets):
    return current.at[offsets].get(mode="promise_in_bounds", unique_indices=True)


def along_z(part, source):
    size = lax.axis_size("zh")
    mine = lax.axis_index("zh")
    best = part
    for shift in (1, size - 1, 2):
        moved = lax.ppermute(part, "zh", [(i, (i + shift) % size) for i in range(size)])
        best = jnp.where((mine - shift) % size == source, moved, best)
    return best


def plane_gather(part):
    planes = lax.axis_size(PLANE)
    whole = jnp.broadcast_to(part[None], (planes,) + part.shape)
    return lax.all_to_all(whole, PLANE, 0, 0).reshape(-1, part.shape[1])


def spread_rows(current, offsets, owner):
    ny, nz, nx = (lax.axis_size(a) for a in STATE)
    here = lax.axis_index(STATE)
    oz = [(o // nx) % nz for o in owner]
    source = [o // (nz * nx) * nx + o % nx for o in owner]
    chosen = jnp.where(here == owner[0], offsets[0], offsets[1])
    received = plane_exchange(pick_rows(current, chosen))
    first = lax.dynamic_index_in_dim(received, source[0], 0, False)
    second = lax.dynamic_index_in_dim(received, source[1], 0, False)
    first = along_z(first, oz[0])
    first, second = lax.optimization_barrier((first, second))
    prior = plane_gather(first)

    def again(_):
        extra = plane_exchange(pick_rows(current, offsets[1]))
        return lax.dynamic_index_in_dim(extra, source[1], 0, False)

    second = lax.cond(owner[0] == owner[1], again, lambda kept: kept, second)
    return prior, along_z(second, oz[1])


def moments_kernel(prior, out, anom_out):
    size, width = prior.shape
    half = size // 2
    value = prior[...]
    anom = value - jnp.sum(value, axis=1, keepdims=True) / width
    anom_out[...] = anom
    for n, (i, j) in enumerate(((0, 0), (1, 0), (1, 1))):
        out[n * half : (n + 1) * half, :] = lax.dot_general(
            anom[i * half : (i + 1) * half],
            anom[j * half : (j + 1) * half],
            (((1,), (1,)), ((), ())),
            precision=finest,
            preferred_element_type=jnp.float32,
        )
    mean = lax.dot_general(
        jnp.ones((GROUP, width), jnp.float32),
        value,
        (((1,), (1,)), ((), ())),
        precision=finest,
        preferred_element_type=jnp.float32,
    ) / width
    row = lax.broadcasted_iota(jnp.int32, (GROUP, half), 0)
    out[3 * half :, :] = jnp.where(
        row == 0, mean[:, :half], jnp.where(row == 1, mean[:, half:], 0.0)
    )


def moments(prior):
    size = prior.shape[0]
    return pl.pallas_call(
        moments_kernel,
        out_shape=(
            jax.ShapeDtypeStruct((3 * size // 2 + GROUP, size // 2), jnp.float32),
            jax.ShapeDtypeStruct(prior.shape, jnp.float32),
        ),
        compiler_params=pltpu.CompilerParams(vmem_limit_bytes=24 << 20),
        cost_estimate=pl.CostEstimate(
            flops=6 * size * size * prior.shape[1] * 2,
            bytes_accessed=4 * size * prior.shape[1],
            transcendentals=0,
        ),
    )(prior)


def merged(mine, other, count):
    half = mine.shape[1]
    delta = mine[3 * half :] - other[3 * half :]
    row = lax.broadcasted_iota(jnp.int32, delta.shape, 0)
    parts = [jnp.where(row == 0, jnp.broadcast_to(delta[i : i + 1], delta.shape), 0.0) for i in (0, 1)]
    out = []
    for n, (i, j) in enumerate(((0, 0), (1, 0), (1, 1))):
        place = slice(n * half, (n + 1) * half)
        outer = lax.dot_general(
            parts[i],
            parts[j],
            (((0,), (0,)), ((), ())),
            precision=finest,
            preferred_element_type=jnp.float32,
        )
        out.append(mine[place] + other[place] + outer * (count / 2))
    out.append((mine[3 * half :] + other[3 * half :]) / 2)
    return out


def merge_kernel(count, mine, other, out):
    half = mine.shape[1]
    parts = merged(mine[...], other[...], count)
    for n in range(3):
        out[n * half : (n + 1) * half, :] = parts[n]
    out[3 * half :, :] = parts[3]


def merge(mine, other, count):
    def body(*refs):
        merge_kernel(count, *refs)

    return pl.pallas_call(
        body,
        out_shape=jax.ShapeDtypeStruct(mine.shape, jnp.float32),
        compiler_params=pltpu.CompilerParams(vmem_limit_bytes=16 << 20),
    )(mine, other)


def inverse_kernel(members, states, reach, mine, other, var_row, off_col, off_row, out):
    half = LANES
    size = 2 * half
    tiles = 2
    parts = merged(mine[...], other[...], members // 2)
    square = ((parts[0], parts[1]), (parts[1].T, parts[2]))
    rows = lax.broadcasted_iota(jnp.int32, (half, half), 0)
    lanes = lax.broadcasted_iota(jnp.int32, (half, half), 1)
    for t in range(tiles):
        cols = slice(t * half, (t + 1) * half)
        for i in range(tiles):
            place = slice(i * half, (i + 1) * half)
            cov = cycle_taper(off_col[place], off_row[:, cols], states, reach) * (
                square[t][i] / (members - 1)
            )
            if i == t:
                cov = cov + jnp.where(rows == lanes, var_row[:, cols], 0.0)
            out[t, place, :] = cov
    row = lax.broadcasted_iota(jnp.int32, (STEP, half), 0)
    lane = lax.broadcasted_iota(jnp.int32, (STEP, half), 1)
    wide = lax.broadcasted_iota(jnp.int32, (size, half), 1)

    def over(x):
        return jnp.broadcast_to(x, (STEP, half))

    current = [out[q, 0:STEP, :] for q in range(tiles)]
    for at in range(0, size, STEP):
        t, base = divmod(at, half)
        inside = (lane >= base) & (lane < base + STEP)
        unit = (lane - base == row).astype(jnp.float32)
        columns = [over(current[t][:, base + j : base + j + 1]) for j in range(STEP)]
        pivots = [jnp.where(inside, unit, x) if q == t else x for q, x in enumerate(current)]
        last = at + STEP == size
        if not last:
            ahead = [out[q, at + STEP : at + 2 * STEP, :] for q in range(tiles)]
            factors = [over(ahead[t][:, base + j : base + j + 1]) for j in range(STEP)]
        for k in range(STEP):
            inv = 1.0 / over(columns[k][k : k + 1])
            factor = columns[k]
            on_row = row == k

            def eliminate(x):
                scaled = over(x[k : k + 1]) * inv
                return jnp.where(on_row, scaled, x - factor * scaled)

            for j in range(k + 1, STEP):
                columns[j] = eliminate(columns[j])
            pivots = [eliminate(x) for x in pivots]
        if not last:
            current = []
            for q in range(tiles):
                acc = jnp.where(inside, 0.0, ahead[q]) if q == t else ahead[q]
                for j in range(STEP):
                    acc = acc - factors[j] * over(pivots[q][j : j + 1])
                current.append(acc)
        panel = out[t, :, :][:, base : base + STEP]
        for q in range(tiles):
            old = out[q]
            if q == t:
                old = jnp.where((wide >= base) & (wide < base + STEP), 0.0, old)
            out[q] = old - jnp.dot(
                panel, pivots[q], precision=finest, preferred_element_type=jnp.float32
            )
        for q in range(tiles):
            out[q, at : at + STEP, :] = pivots[q]


def inverse_cov(mine, other, variance, places, members, states, reach):
    size = places.shape[0]

    def body(*refs):
        inverse_kernel(members, states, reach, *refs)

    tiled = pl.pallas_call(
        body,
        out_shape=jax.ShapeDtypeStruct((size // LANES, size, LANES), jnp.float32),
        compiler_params=pltpu.CompilerParams(vmem_limit_bytes=16 << 20),
        cost_estimate=pl.CostEstimate(flops=8 * 10**9, bytes_accessed=1 << 20, transcendentals=0),
    )(mine, other, variance[None, :], places[:, None], places[None, :])
    return jnp.concatenate([tiled[t] for t in range(size // LANES)], axis=1)


def local(ensemble, obs_values, obs_noise, obs_var, obs_offset, owner):
    rows, width = ensemble.shape
    members = width * lax.axis_size(ENS)
    states = rows * lax.axis_size(STATE)
    reach = states // 4
    here = lax.axis_index(STATE)
    owner = [owner[b] for b in range(NB)]
    positions = here * rows + jnp.arange(rows, dtype=jnp.int32)
    places = [owner[b] * rows + obs_offset[b] for b in range(NB)]

    def misfit(batch, prior):
        return (
            obs_values[batch][:, None]
            + jnp.sqrt(obs_var[batch])[:, None] * obs_noise[batch].astype(jnp.float32)
            - prior
        )

    def products(x, anom):
        return jnp.einsum("sm,pm->sp", x, anom, precision=close), jnp.sum(x, axis=1)

    def shifted(cross, total, shift):
        return pair_sum(cross + total[:, None] * shift)

    def gain_of(cross, spots, batch, inverse):
        gain = cycle_taper(spots[:, None], places[batch][None, :], states, reach) * (
            cross / (members - 1)
        )
        return jnp.dot(gain, inverse, precision=close)

    def update(x, gain, values):
        return x + jnp.dot(gain, values, precision=close)

    def statistics(prior):
        stats, anom = moments(prior)
        own = stats[-GROUP:][:2]
        stats = merge(stats, swap(stats, "core"), width)
        return own, anom, stats

    def shift_of(own, stats, other):
        whole = ((stats[-GROUP:] + other[-GROUP:]) / 2)[:2]
        return (own - whole).reshape(1, 2 * own.shape[1])

    prior, second = spread_rows(ensemble, obs_offset, owner)
    own, anom, stats = statistics(prior)
    other = swap(stats, "zl")
    stats, second = lax.optimization_barrier((stats, second))
    later = plane_gather(second)
    mine = products(ensemble, anom)
    shift = shift_of(own, stats, other)
    inverse = inverse_cov(stats, other, obs_var[0], places[0], members, states, reach)
    mine, inverse = lax.optimization_barrier((mine, inverse))
    kept = shifted(*mine, shift)
    moved = swap(kept, "zl")
    theirs = shifted(*products(later, anom), shift)
    theirs = whole_sum(theirs, swap(theirs, "zl"))
    values = misfit(0, prior)
    prior = update(later, gain_of(theirs, places[1], 0, inverse), values)
    gain = gain_of(whole_sum(kept, moved), positions, 0, inverse)
    current = update(ensemble, gain, values)

    own, anom, stats = statistics(prior)
    other = swap(stats, "zl")
    cross = products(current, anom)
    kept = shifted(*cross, shift_of(own, stats, other))
    stats, kept = lax.optimization_barrier((stats, kept))
    moved = swap(kept, "zl")
    inverse = inverse_cov(stats, other, obs_var[1], places[1], members, states, reach)
    moved, inverse = lax.optimization_barrier((moved, inverse))
    gain = gain_of(whole_sum(kept, moved), positions, 1, inverse)
    return update(current, gain, misfit(1, prior))


def solution(mesh):
    ens, state = mesh.devices.shape
    fine = Mesh(
        mesh.devices.reshape(2, ens // 2, 4, state // 16, 4), ("zl", "core", "y", "zh", "x")
    )
    in_specs = (P(STATE, ENS), P(), P(None, None, ENS), P(), P(), P())
    return jax.shard_map(
        local, mesh=fine, in_specs=in_specs, out_specs=P(STATE, ENS), check_vma=False
    )
```

```python
import jax
import jax.numpy as jnp
from jax import lax
from jax.experimental import pallas as pl
from jax.experimental.pallas import tpu as pltpu
from jax.sharding import Mesh, PartitionSpec as P

NB = 2
finest = lax.Precision.HIGHEST
close = lax.Precision.HIGH
ENS = ("zl", "core")
PLANE = ("y", "x")
STATE = ("y", "zh", "x")
GROUP = 8
STEP = 16
LANES = 128


def cycle_taper(first, second, total, reach):
    distance = jnp.abs(first - second)
    distance = jnp.minimum(distance, total - distance).astype(jnp.float32)
    ratio = distance / jnp.float32(reach)
    return 1.0 / (1.0 + ratio * ratio)


def swap(value, axis):
    return lax.ppermute(value, axis, [(0, 1), (1, 0)])


def pair_sum(value):
    half = value.shape[0] // 2
    first = lax.axis_index("core") == 0
    top, bottom = value[:half], value[half:]
    return jnp.where(first, top, bottom) + swap(jnp.where(first, bottom, top), "core")


def whole_sum(kept, moved):
    first = lax.axis_index("core") == 0
    kept = kept + moved
    other = swap(kept, "core")
    return jnp.concatenate(
        [jnp.where(first, kept, other), jnp.where(first, other, kept)], axis=0
    )


def plane_exchange(rows):
    planes = lax.axis_size(PLANE)
    blocks = rows.reshape(planes, rows.shape[0] // planes, rows.shape[1])
    return lax.all_to_all(blocks, PLANE, 0, 0)


def pick_kernel(here, owner, offsets, value, out):
    chosen = jnp.where(here[0] == owner[0], offsets[0:1, :], offsets[1:2, :])
    rows = lax.broadcasted_iota(jnp.int32, (value.shape[0], chosen.shape[1]), 0)
    hot = (rows == chosen).astype(jnp.float32).astype(jnp.bfloat16)
    rest = value[...]
    total = None
    for _ in range(3):
        part = rest.astype(jnp.bfloat16)
        rest = rest - part.astype(jnp.float32)
        term = lax.dot_general(
            hot, part, (((0,), (0,)), ((), ())), preferred_element_type=jnp.float32
        )
        total = term if total is None else total + term
    out[...] = total


def pick_rows(current, offsets, here, owner):
    rows, width = current.shape
    size = offsets.shape[1]
    block = width // 2
    return pl.pallas_call(
        pick_kernel,
        grid=(2,),
        in_specs=[
            pl.BlockSpec(memory_space=pltpu.SMEM),
            pl.BlockSpec(memory_space=pltpu.SMEM),
            pl.BlockSpec((NB, size), lambda i: (0, 0)),
            pl.BlockSpec((rows, block), lambda i: (0, i)),
        ],
        out_specs=pl.BlockSpec((size, block), lambda i: (0, i)),
        out_shape=jax.ShapeDtypeStruct((size, width), jnp.float32),
        compiler_params=pltpu.CompilerParams(vmem_limit_bytes=24 << 20),
    )(here.astype(jnp.int32).reshape(1), owner, offsets, current)


def along_z(part, source):
    size = lax.axis_size("zh")
    mine = lax.axis_index("zh")
    best = part
    for shift in (1, size - 1, 2):
        moved = lax.ppermute(part, "zh", [(i, (i + shift) % size) for i in range(size)])
        best = jnp.where((mine - shift) % size == source, moved, best)
    return best


def plane_copies(part):
    return jnp.broadcast_to(part[None], (lax.axis_size(PLANE),) + part.shape)


def plane_gather(whole):
    return lax.all_to_all(whole, PLANE, 0, 0).reshape(-1, whole.shape[2])


def spread_rows(current, offsets, owners):
    ny, nz, nx = (lax.axis_size(a) for a in STATE)
    here = lax.axis_index(STATE)
    owner = [owners[b] for b in range(NB)]
    oz = [(o // nx) % nz for o in owner]
    source = [o // (nz * nx) * nx + o % nx for o in owner]
    received = plane_exchange(pick_rows(current, offsets, here, owners))
    first = lax.dynamic_index_in_dim(received, source[0], 0, False)
    second = lax.dynamic_index_in_dim(received, source[1], 0, False)
    first = along_z(first, oz[0])
    first, second = lax.optimization_barrier((first, second))
    prior = plane_gather(plane_copies(first))

    def again(_):
        extra = plane_exchange(pick_rows(current, offsets, here - lax.axis_size(STATE), owners))
        return lax.dynamic_index_in_dim(extra, source[1], 0, False)

    second = lax.cond(owner[0] == owner[1], again, lambda kept: kept, second)
    return prior, along_z(second, oz[1])


def moments_kernel(prior, out, anom_out):
    size, width = prior.shape
    half = size // 2
    value = prior[...]
    mean = jnp.sum(value, axis=1, keepdims=True) / width
    anom = value - mean
    anom_out[...] = anom
    square = lax.dot_general(
        anom,
        anom,
        (((1,), (1,)), ((), ())),
        precision=finest,
        preferred_element_type=jnp.float32,
    )
    out[:half, :] = square[:half, :half]
    out[half : 2 * half, :] = square[half:, :half]
    out[2 * half : 3 * half, :] = square[half:, half:]
    row = lax.broadcasted_iota(jnp.int32, (GROUP, half), 0)
    low, high = (
        jnp.broadcast_to(mean[i * half : (i + 1) * half], (half, half)).T[:GROUP]
        for i in range(2)
    )
    out[3 * half :, :] = jnp.where(row == 0, low, jnp.where(row == 1, high, 0.0))


def moments(prior):
    size = prior.shape[0]
    return pl.pallas_call(
        moments_kernel,
        out_shape=(
            jax.ShapeDtypeStruct((3 * size // 2 + GROUP, size // 2), jnp.float32),
            jax.ShapeDtypeStruct(prior.shape, jnp.float32),
        ),
        compiler_params=pltpu.CompilerParams(vmem_limit_bytes=24 << 20),
        cost_estimate=pl.CostEstimate(
            flops=6 * size * size * prior.shape[1] * 2,
            bytes_accessed=4 * size * prior.shape[1],
            transcendentals=0,
        ),
    )(prior)


def merged(mine, other, count):
    half = mine.shape[1]
    delta = mine[3 * half :] - other[3 * half :]
    row = lax.broadcasted_iota(jnp.int32, delta.shape, 0)
    parts = [jnp.where(row == 0, jnp.broadcast_to(delta[i : i + 1], delta.shape), 0.0) for i in (0, 1)]
    out = []
    for n, (i, j) in enumerate(((0, 0), (1, 0), (1, 1))):
        place = slice(n * half, (n + 1) * half)
        outer = lax.dot_general(
            parts[i],
            parts[j],
            (((0,), (0,)), ((), ())),
            precision=finest,
            preferred_element_type=jnp.float32,
        )
        out.append(mine[place] + other[place] + outer * (count / 2))
    out.append((mine[3 * half :] + other[3 * half :]) / 2)
    return out


def merge_kernel(count, mine, other, out):
    half = mine.shape[1]
    parts = merged(mine[...], other[...], count)
    for n in range(3):
        out[n * half : (n + 1) * half, :] = parts[n]
    out[3 * half :, :] = parts[3]


def merge(mine, other, count):
    def body(*refs):
        merge_kernel(count, *refs)

    return pl.pallas_call(
        body,
        out_shape=jax.ShapeDtypeStruct(mine.shape, jnp.float32),
        compiler_params=pltpu.CompilerParams(vmem_limit_bytes=16 << 20),
    )(mine, other)


def inverse_kernel(members, states, reach, mine, other, var_row, off_col, off_row, out):
    half = LANES
    size = 2 * half
    tiles = 2
    parts = merged(mine[...], other[...], members // 2)
    square = ((parts[0], parts[1]), (parts[1].T, parts[2]))
    rows = lax.broadcasted_iota(jnp.int32, (half, half), 0)
    lanes = lax.broadcasted_iota(jnp.int32, (half, half), 1)
    for t in range(tiles):
        cols = slice(t * half, (t + 1) * half)
        for i in range(tiles):
            place = slice(i * half, (i + 1) * half)
            cov = cycle_taper(off_col[place], off_row[:, cols], states, reach) * (
                square[t][i] / (members - 1)
            )
            if i == t:
                cov = cov + jnp.where(rows == lanes, var_row[:, cols], 0.0)
            out[t, place, :] = cov
    row = lax.broadcasted_iota(jnp.int32, (STEP, half), 0)
    lane = lax.broadcasted_iota(jnp.int32, (STEP, half), 1)
    wide = lax.broadcasted_iota(jnp.int32, (size, half), 1)

    def over(x):
        return jnp.broadcast_to(x, (STEP, half))

    current = [out[q, 0:STEP, :] for q in range(tiles)]
    for at in range(0, size, STEP):
        t, base = divmod(at, half)
        inside = (lane >= base) & (lane < base + STEP)
        unit = (lane - base == row).astype(jnp.float32)
        columns = [over(current[t][:, base + j : base + j + 1]) for j in range(STEP)]
        pivots = [jnp.where(inside, unit, x) if q == t else x for q, x in enumerate(current)]
        last = at + STEP == size
        if not last:
            ahead = [out[q, at + STEP : at + 2 * STEP, :] for q in range(tiles)]
            factors = [over(ahead[t][:, base + j : base + j + 1]) for j in range(STEP)]
        for k in range(STEP):
            inv = 1.0 / over(columns[k][k : k + 1])
            factor = columns[k]
            on_row = row == k

            def eliminate(x):
                scaled = over(x[k : k + 1]) * inv
                return jnp.where(on_row, scaled, x - factor * scaled)

            for j in range(k + 1, STEP):
                columns[j] = eliminate(columns[j])
            pivots = [eliminate(x) for x in pivots]
        if not last:
            current = []
            for q in range(tiles):
                acc = jnp.where(inside, 0.0, ahead[q]) if q == t else ahead[q]
                for j in range(STEP):
                    acc = acc - factors[j] * over(pivots[q][j : j + 1])
                current.append(acc)
        panel = out[t, :, :][:, base : base + STEP]
        for q in range(tiles):
            old = out[q]
            if q == t:
                old = jnp.where((wide >= base) & (wide < base + STEP), 0.0, old)
            out[q] = old - jnp.dot(
                panel, pivots[q], precision=finest, preferred_element_type=jnp.float32
            )
        for q in range(tiles):
            out[q, at : at + STEP, :] = pivots[q]


def inverse_cov(mine, other, variance, places, members, states, reach):
    size = places.shape[0]

    def body(*refs):
        inverse_kernel(members, states, reach, *refs)

    tiled = pl.pallas_call(
        body,
        out_shape=jax.ShapeDtypeStruct((size // LANES, size, LANES), jnp.float32),
        compiler_params=pltpu.CompilerParams(vmem_limit_bytes=16 << 20),
        cost_estimate=pl.CostEstimate(flops=8 * 10**9, bytes_accessed=1 << 20, transcendentals=0),
    )(mine, other, variance[None, :], places[:, None], places[None, :])
    return jnp.concatenate([tiled[t] for t in range(size // LANES)], axis=1)


def local(ensemble, obs_values, obs_noise, obs_var, obs_offset, owner):
    rows, width = ensemble.shape
    members = width * lax.axis_size(ENS)
    states = rows * lax.axis_size(STATE)
    reach = states // 4
    here = lax.axis_index(STATE)
    positions = here * rows + jnp.arange(rows, dtype=jnp.int32)
    places = [owner[b] * rows + obs_offset[b] for b in range(NB)]

    def misfit(batch, prior):
        return (
            obs_values[batch][:, None]
            + jnp.sqrt(obs_var[batch])[:, None] * obs_noise[batch].astype(jnp.float32)
            - prior
        )

    def products(x, anom):
        return jnp.einsum("sm,pm->sp", x, anom, precision=close), jnp.sum(x, axis=1)

    def shifted(cross, total, shift):
        return pair_sum(cross + total[:, None] * shift)

    def gain_of(cross, spots, batch, inverse):
        gain = cycle_taper(spots[:, None], places[batch][None, :], states, reach) * (
            cross / (members - 1)
        )
        return jnp.dot(gain, inverse, precision=close)

    def update(x, gain, values):
        return x + jnp.dot(gain, values, precision=close)

    def statistics(prior):
        stats, anom = moments(prior)
        own = stats[-GROUP:][:2]
        stats = merge(stats, swap(stats, "core"), width)
        return own, anom, stats

    def shift_of(own, stats, other):
        whole = ((stats[-GROUP:] + other[-GROUP:]) / 2)[:2]
        return (own - whole).reshape(1, 2 * own.shape[1])

    prior, second = spread_rows(ensemble, obs_offset, owner)
    prior, second = lax.optimization_barrier((prior, plane_copies(second)))
    later = plane_gather(second)
    own, anom, stats = statistics(prior)
    other = swap(stats, "zl")
    mine = products(ensemble, anom)
    shift = shift_of(own, stats, other)
    inverse = inverse_cov(stats, other, obs_var[0], places[0], members, states, reach)
    centered = anom + shift.reshape(-1, 1)
    values = misfit(0, prior)
    mine, centered, values, inverse = lax.optimization_barrier((mine, centered, values, inverse))
    theirs = pair_sum(jnp.einsum("sm,pm->sp", later, centered, precision=close))
    theirs, mine = lax.optimization_barrier((theirs, mine))
    theirs = whole_sum(theirs, swap(theirs, "zl"))
    kept = shifted(*mine, shift)
    moved = swap(kept, "zl")
    prior = update(later, gain_of(theirs, places[1], 0, inverse), values)
    gain = gain_of(whole_sum(kept, moved), positions, 0, inverse)
    current = update(ensemble, gain, values)

    own, anom, stats = statistics(prior)
    other = swap(stats, "zl")
    cross = products(current, anom)
    kept = shifted(*cross, shift_of(own, stats, other))
    stats, kept = lax.optimization_barrier((stats, kept))
    moved = swap(kept, "zl")
    inverse = inverse_cov(stats, other, obs_var[1], places[1], members, states, reach)
    moved, inverse = lax.optimization_barrier((moved, inverse))
    gain = gain_of(whole_sum(kept, moved), positions, 1, inverse)
    return update(current, gain, misfit(1, prior))


def solution(mesh):
    ens, state = mesh.devices.shape
    fine = Mesh(
        mesh.devices.reshape(2, ens // 2, 4, state // 16, 4), ("zl", "core", "y", "zh", "x")
    )
    in_specs = (P(STATE, ENS), P(), P(None, None, ENS), P(), P(), P())
    return jax.shard_map(
        local, mesh=fine, in_specs=in_specs, out_specs=P(STATE, ENS), check_vma=False
    )
```

```python
import jax
import jax.numpy as jnp
from jax import lax
from jax.experimental import pallas as pl
from jax.experimental.pallas import tpu as pltpu
from jax.sharding import Mesh, PartitionSpec as P

NB = 2
finest = lax.Precision.HIGHEST
close = lax.Precision.HIGH
ENS = ("zl", "core")
PLANE = ("y", "x")
STATE = ("y", "zh", "x")
GROUP = 8
STEP = 16
LANES = 128


def cycle_taper(first, second, total, reach):
    distance = jnp.abs(first - second)
    distance = jnp.minimum(distance, total - distance).astype(jnp.float32)
    ratio = distance / jnp.float32(reach)
    return 1.0 / (1.0 + ratio * ratio)


def swap(value, axis):
    return lax.ppermute(value, axis, [(0, 1), (1, 0)])


def pair_sum(value):
    half = value.shape[0] // 2
    first = lax.axis_index("core") == 0
    top, bottom = value[:half], value[half:]
    return jnp.where(first, top, bottom) + swap(jnp.where(first, bottom, top), "core")


def whole_sum(kept, moved):
    first = lax.axis_index("core") == 0
    kept = kept + moved
    other = swap(kept, "core")
    return jnp.concatenate(
        [jnp.where(first, kept, other), jnp.where(first, other, kept)], axis=0
    )


def plane_exchange(rows):
    planes = lax.axis_size(PLANE)
    blocks = rows.reshape(planes, rows.shape[0] // planes, rows.shape[1])
    return lax.all_to_all(blocks, PLANE, 0, 0)


def pick_kernel(here, owner, offsets, value, out):
    chosen = jnp.where(here[0] == owner[0], offsets[0:1, :], offsets[1:2, :])
    rows = lax.broadcasted_iota(jnp.int32, (value.shape[0], chosen.shape[1]), 0)
    hot = (rows == chosen).astype(jnp.float32).astype(jnp.bfloat16)
    rest = value[...]
    total = None
    for _ in range(3):
        part = rest.astype(jnp.bfloat16)
        rest = rest - part.astype(jnp.float32)
        term = lax.dot_general(
            hot, part, (((0,), (0,)), ((), ())), preferred_element_type=jnp.float32
        )
        total = term if total is None else total + term
    out[...] = total


def pick_rows(current, offsets, here, owner):
    rows, width = current.shape
    size = offsets.shape[1]
    block = width // 2
    return pl.pallas_call(
        pick_kernel,
        grid=(2,),
        in_specs=[
            pl.BlockSpec(memory_space=pltpu.SMEM),
            pl.BlockSpec(memory_space=pltpu.SMEM),
            pl.BlockSpec((NB, size), lambda i: (0, 0)),
            pl.BlockSpec((rows, block), lambda i: (0, i)),
        ],
        out_specs=pl.BlockSpec((size, block), lambda i: (0, i)),
        out_shape=jax.ShapeDtypeStruct((size, width), jnp.float32),
        compiler_params=pltpu.CompilerParams(vmem_limit_bytes=24 << 20),
    )(here.astype(jnp.int32).reshape(1), owner, offsets, current)


def along_z(part, source):
    size = lax.axis_size("zh")
    mine = lax.axis_index("zh")
    best = part
    for shift in (1, size - 1, 2):
        moved = lax.ppermute(part, "zh", [(i, (i + shift) % size) for i in range(size)])
        best = jnp.where((mine - shift) % size == source, moved, best)
    return best


def plane_copies(part):
    return jnp.broadcast_to(part[None], (lax.axis_size(PLANE),) + part.shape)


def plane_gather(whole):
    return lax.all_to_all(whole, PLANE, 0, 0).reshape(-1, whole.shape[2])


def spread_rows(current, offsets, owners):
    ny, nz, nx = (lax.axis_size(a) for a in STATE)
    here = lax.axis_index(STATE)
    owner = [owners[b] for b in range(NB)]
    oz = [(o // nx) % nz for o in owner]
    source = [o // (nz * nx) * nx + o % nx for o in owner]
    received = plane_exchange(pick_rows(current, offsets, here, owners))
    first = lax.dynamic_index_in_dim(received, source[0], 0, False)
    second = lax.dynamic_index_in_dim(received, source[1], 0, False)
    first = along_z(first, oz[0])
    first, second = lax.optimization_barrier((first, second))
    prior = plane_gather(plane_copies(first))

    def again(_):
        extra = plane_exchange(pick_rows(current, offsets, here - lax.axis_size(STATE), owners))
        return lax.dynamic_index_in_dim(extra, source[1], 0, False)

    second = lax.cond(owner[0] == owner[1], again, lambda kept: kept, second)
    return prior, along_z(second, oz[1])


def moments_kernel(prior, out, anom_out):
    size, width = prior.shape
    half = size // 2
    value = prior[...]
    mean = jnp.sum(value, axis=1, keepdims=True) / width
    anom = value - mean
    anom_out[...] = anom
    square = lax.dot_general(
        anom,
        anom,
        (((1,), (1,)), ((), ())),
        precision=finest,
        preferred_element_type=jnp.float32,
    )
    out[:half, :] = square[:half, :half]
    out[half : 2 * half, :] = square[half:, :half]
    out[2 * half : 3 * half, :] = square[half:, half:]
    row = lax.broadcasted_iota(jnp.int32, (GROUP, half), 0)
    low, high = (
        jnp.broadcast_to(mean[i * half : (i + 1) * half], (half, half)).T[:GROUP]
        for i in range(2)
    )
    out[3 * half :, :] = jnp.where(row == 0, low, jnp.where(row == 1, high, 0.0))


def moments(prior):
    size = prior.shape[0]
    return pl.pallas_call(
        moments_kernel,
        out_shape=(
            jax.ShapeDtypeStruct((3 * size // 2 + GROUP, size // 2), jnp.float32),
            jax.ShapeDtypeStruct(prior.shape, jnp.float32),
        ),
        compiler_params=pltpu.CompilerParams(vmem_limit_bytes=24 << 20),
        cost_estimate=pl.CostEstimate(
            flops=6 * size * size * prior.shape[1] * 2,
            bytes_accessed=4 * size * prior.shape[1],
            transcendentals=0,
        ),
    )(prior)


def merged(mine, other, count):
    half = mine.shape[1]
    delta = mine[3 * half :] - other[3 * half :]
    row = lax.broadcasted_iota(jnp.int32, delta.shape, 0)
    parts = [jnp.where(row == 0, jnp.broadcast_to(delta[i : i + 1], delta.shape), 0.0) for i in (0, 1)]
    out = []
    for n, (i, j) in enumerate(((0, 0), (1, 0), (1, 1))):
        place = slice(n * half, (n + 1) * half)
        outer = lax.dot_general(
            parts[i],
            parts[j],
            (((0,), (0,)), ((), ())),
            precision=finest,
            preferred_element_type=jnp.float32,
        )
        out.append(mine[place] + other[place] + outer * (count / 2))
    out.append((mine[3 * half :] + other[3 * half :]) / 2)
    return out


def merge_kernel(count, mine, other, out):
    half = mine.shape[1]
    parts = merged(mine[...], other[...], count)
    for n in range(3):
        out[n * half : (n + 1) * half, :] = parts[n]
    out[3 * half :, :] = parts[3]


def merge(mine, other, count):
    def body(*refs):
        merge_kernel(count, *refs)

    return pl.pallas_call(
        body,
        out_shape=jax.ShapeDtypeStruct(mine.shape, jnp.float32),
        compiler_params=pltpu.CompilerParams(vmem_limit_bytes=16 << 20),
    )(mine, other)


def inverse_kernel(members, states, reach, mine, other, var_row, off_col, off_row, out):
    half = LANES
    size = 2 * half
    tiles = 2
    parts = merged(mine[...], other[...], members // 2)
    square = ((parts[0], parts[1]), (parts[1].T, parts[2]))
    rows = lax.broadcasted_iota(jnp.int32, (half, half), 0)
    lanes = lax.broadcasted_iota(jnp.int32, (half, half), 1)
    for t in range(tiles):
        cols = slice(t * half, (t + 1) * half)
        for i in range(tiles):
            place = slice(i * half, (i + 1) * half)
            cov = cycle_taper(off_col[place], off_row[:, cols], states, reach) * (
                square[t][i] / (members - 1)
            )
            if i == t:
                cov = cov + jnp.where(rows == lanes, var_row[:, cols], 0.0)
            out[t, place, :] = cov
    row = lax.broadcasted_iota(jnp.int32, (STEP, half), 0)
    lane = lax.broadcasted_iota(jnp.int32, (STEP, half), 1)
    wide = lax.broadcasted_iota(jnp.int32, (size, half), 1)

    def over(x):
        return jnp.broadcast_to(x, (STEP, half))

    current = [out[q, 0:STEP, :] for q in range(tiles)]
    for at in range(0, size, STEP):
        t, base = divmod(at, half)
        inside = (lane >= base) & (lane < base + STEP)
        unit = (lane - base == row).astype(jnp.float32)
        columns = [over(current[t][:, base + j : base + j + 1]) for j in range(STEP)]
        pivots = [jnp.where(inside, unit, x) if q == t else x for q, x in enumerate(current)]
        last = at + STEP == size
        if not last:
            ahead = [out[q, at + STEP : at + 2 * STEP, :] for q in range(tiles)]
            factors = [over(ahead[t][:, base + j : base + j + 1]) for j in range(STEP)]
        for k in range(STEP):
            inv = 1.0 / over(columns[k][k : k + 1])
            factor = columns[k]
            on_row = row == k

            def eliminate(x):
                scaled = over(x[k : k + 1]) * inv
                return jnp.where(on_row, scaled, x - factor * scaled)

            for j in range(k + 1, STEP):
                columns[j] = eliminate(columns[j])
            pivots = [eliminate(x) for x in pivots]
        if not last:
            current = []
            for q in range(tiles):
                acc = jnp.where(inside, 0.0, ahead[q]) if q == t else ahead[q]
                for j in range(STEP):
                    acc = acc - factors[j] * over(pivots[q][j : j + 1])
                current.append(acc)
        panel = out[t, :, :][:, base : base + STEP]
        for q in range(tiles):
            old = out[q]
            if q == t:
                old = jnp.where((wide >= base) & (wide < base + STEP), 0.0, old)
            out[q] = old - jnp.dot(
                panel, pivots[q], precision=finest, preferred_element_type=jnp.float32
            )
        for q in range(tiles):
            out[q, at : at + STEP, :] = pivots[q]


def inverse_cov(mine, other, variance, places, members, states, reach):
    size = places.shape[0]

    def body(*refs):
        inverse_kernel(members, states, reach, *refs)

    tiled = pl.pallas_call(
        body,
        out_shape=jax.ShapeDtypeStruct((size // LANES, size, LANES), jnp.float32),
        compiler_params=pltpu.CompilerParams(vmem_limit_bytes=16 << 20),
        cost_estimate=pl.CostEstimate(flops=8 * 10**9, bytes_accessed=1 << 20, transcendentals=0),
    )(mine, other, variance[None, :], places[:, None], places[None, :])
    return jnp.concatenate([tiled[t] for t in range(size // LANES)], axis=1)


def local(ensemble, obs_values, obs_noise, obs_var, obs_offset, owner):
    rows, width = ensemble.shape
    members = width * lax.axis_size(ENS)
    states = rows * lax.axis_size(STATE)
    reach = states // 4
    here = lax.axis_index(STATE)
    positions = here * rows + jnp.arange(rows, dtype=jnp.int32)
    places = [owner[b] * rows + obs_offset[b] for b in range(NB)]

    def misfit(batch, prior):
        return (
            obs_values[batch][:, None]
            + jnp.sqrt(obs_var[batch])[:, None] * obs_noise[batch].astype(jnp.float32)
            - prior
        )

    def products(x, anom):
        return jnp.einsum("sm,pm->sp", x, anom, precision=close), jnp.sum(x, axis=1)

    def shifted(cross, total, shift):
        return pair_sum(cross + total[:, None] * shift)

    def gain_of(cross, spots, batch, inverse):
        gain = cycle_taper(spots[:, None], places[batch][None, :], states, reach) * (
            cross / (members - 1)
        )
        return jnp.dot(gain, inverse, precision=close)

    def update(x, gain, values):
        return x + jnp.dot(gain, values, precision=close)

    def statistics(prior):
        stats, anom = moments(prior)
        own = stats[-GROUP:][:2]
        stats = merge(stats, swap(stats, "core"), width)
        return own, anom, stats

    def shift_of(own, stats, other):
        whole = ((stats[-GROUP:] + other[-GROUP:]) / 2)[:2]
        return (own - whole).reshape(1, 2 * own.shape[1])

    prior, second = spread_rows(ensemble, obs_offset, owner)
    prior, second = lax.optimization_barrier((prior, plane_copies(second)))
    later = plane_gather(second)
    own, anom, stats = statistics(prior)
    other = swap(stats, "zl")
    mine = products(ensemble, anom)
    shift = shift_of(own, stats, other)
    inverse = inverse_cov(stats, other, obs_var[0], places[0], members, states, reach)
    centered = anom + shift.reshape(-1, 1)
    values = misfit(0, prior)
    mine, centered, values, inverse = lax.optimization_barrier((mine, centered, values, inverse))
    theirs = pair_sum(jnp.einsum("sm,pm->sp", later, centered, precision=close))
    kept = shifted(*mine, shift)
    theirs, kept = lax.optimization_barrier((theirs, kept))
    joined = swap(theirs, "zl")
    moved = swap(kept, "zl")
    theirs = whole_sum(theirs, joined)
    prior = update(later, gain_of(theirs, places[1], 0, inverse), values)
    gain = gain_of(whole_sum(kept, moved), positions, 0, inverse)
    current = update(ensemble, gain, values)

    own, anom, stats = statistics(prior)
    other = swap(stats, "zl")
    cross = products(current, anom)
    kept = shifted(*cross, shift_of(own, stats, other))
    stats, kept = lax.optimization_barrier((stats, kept))
    moved = swap(kept, "zl")
    inverse = inverse_cov(stats, other, obs_var[1], places[1], members, states, reach)
    moved, inverse = lax.optimization_barrier((moved, inverse))
    gain = gain_of(whole_sum(kept, moved), positions, 1, inverse)
    return update(current, gain, misfit(1, prior))


def solution(mesh):
    ens, state = mesh.devices.shape
    fine = Mesh(
        mesh.devices.reshape(2, ens // 2, 4, state // 16, 4), ("zl", "core", "y", "zh", "x")
    )
    in_specs = (P(STATE, ENS), P(), P(None, None, ENS), P(), P(), P())
    return jax.shard_map(
        local, mesh=fine, in_specs=in_specs, out_specs=P(STATE, ENS), check_vma=False
    )
```

```python
import jax
import jax.numpy as jnp
from jax import lax
from jax.experimental import pallas as pl
from jax.experimental.pallas import tpu as pltpu
from jax.sharding import Mesh, PartitionSpec as P

NB = 2
finest = lax.Precision.HIGHEST
close = lax.Precision.HIGH
ENS = ("zl", "core")
PLANE = ("y", "x")
STATE = ("y", "zh", "x")
GROUP = 8
STEP = 16
LANES = 128


def cycle_taper(first, second, total, reach):
    distance = jnp.abs(first - second)
    distance = jnp.minimum(distance, total - distance).astype(jnp.float32)
    ratio = distance / jnp.float32(reach)
    return 1.0 / (1.0 + ratio * ratio)


def swap(value, axis):
    return lax.ppermute(value, axis, [(0, 1), (1, 0)])


def pair_sum(value):
    half = value.shape[0] // 2
    first = lax.axis_index("core") == 0
    top, bottom = value[:half], value[half:]
    return jnp.where(first, top, bottom) + swap(jnp.where(first, bottom, top), "core")


def whole_sum(kept, moved):
    first = lax.axis_index("core") == 0
    kept = kept + moved
    other = swap(kept, "core")
    return jnp.concatenate(
        [jnp.where(first, kept, other), jnp.where(first, other, kept)], axis=0
    )


def plane_exchange(rows):
    planes = lax.axis_size(PLANE)
    blocks = rows.reshape(planes, rows.shape[0] // planes, rows.shape[1])
    return lax.all_to_all(blocks, PLANE, 0, 0)


def pick_kernel(here, owner, offsets, value, out):
    chosen = jnp.where(here[0] == owner[0], offsets[0:1, :], offsets[1:2, :])
    rows = lax.broadcasted_iota(jnp.int32, (value.shape[0], chosen.shape[1]), 0)
    hot = (rows == chosen).astype(jnp.float32).astype(jnp.bfloat16)
    rest = value[...]
    total = None
    for _ in range(3):
        part = rest.astype(jnp.bfloat16)
        rest = rest - part.astype(jnp.float32)
        term = lax.dot_general(
            hot, part, (((0,), (0,)), ((), ())), preferred_element_type=jnp.float32
        )
        total = term if total is None else total + term
    out[...] = total


def pick_rows(current, offsets, here, owner):
    rows, width = current.shape
    size = offsets.shape[1]
    block = width // 2
    return pl.pallas_call(
        pick_kernel,
        grid=(2,),
        in_specs=[
            pl.BlockSpec(memory_space=pltpu.SMEM),
            pl.BlockSpec(memory_space=pltpu.SMEM),
            pl.BlockSpec((NB, size), lambda i: (0, 0)),
            pl.BlockSpec((rows, block), lambda i: (0, i)),
        ],
        out_specs=pl.BlockSpec((size, block), lambda i: (0, i)),
        out_shape=jax.ShapeDtypeStruct((size, width), jnp.float32),
        compiler_params=pltpu.CompilerParams(vmem_limit_bytes=24 << 20),
    )(here.astype(jnp.int32).reshape(1), owner, offsets, current)


def along_z(part, source):
    size = lax.axis_size("zh")
    mine = lax.axis_index("zh")
    best = part
    for shift in (1, size - 1, 2):
        moved = lax.ppermute(part, "zh", [(i, (i + shift) % size) for i in range(size)])
        best = jnp.where((mine - shift) % size == source, moved, best)
    return best


def plane_copies(part):
    return jnp.broadcast_to(part[None], (lax.axis_size(PLANE),) + part.shape)


def plane_gather(whole):
    return lax.all_to_all(whole, PLANE, 0, 0).reshape(-1, whole.shape[2])


def spread_rows(current, offsets, owners):
    ny, nz, nx = (lax.axis_size(a) for a in STATE)
    here = lax.axis_index(STATE)
    owner = [owners[b] for b in range(NB)]
    oz = [(o // nx) % nz for o in owner]
    source = [o // (nz * nx) * nx + o % nx for o in owner]
    received = plane_exchange(pick_rows(current, offsets, here, owners))
    first = lax.dynamic_index_in_dim(received, source[0], 0, False)
    second = lax.dynamic_index_in_dim(received, source[1], 0, False)
    first = along_z(first, oz[0])
    first, second = lax.optimization_barrier((first, second))
    prior = plane_gather(plane_copies(first))

    def again(_):
        extra = plane_exchange(pick_rows(current, offsets, here - lax.axis_size(STATE), owners))
        return lax.dynamic_index_in_dim(extra, source[1], 0, False)

    second = lax.cond(owner[0] == owner[1], again, lambda kept: kept, second)
    return prior, along_z(second, oz[1])


def moments_kernel(prior, out, anom_out):
    size, width = prior.shape
    half = size // 2
    value = prior[...]
    mean = jnp.sum(value, axis=1, keepdims=True) / width
    anom = value - mean
    anom_out[...] = anom
    square = lax.dot_general(
        anom,
        anom,
        (((1,), (1,)), ((), ())),
        precision=finest,
        preferred_element_type=jnp.float32,
    )
    out[:half, :] = square[:half, :half]
    out[half : 2 * half, :] = square[half:, :half]
    out[2 * half : 3 * half, :] = square[half:, half:]
    row = lax.broadcasted_iota(jnp.int32, (GROUP, half), 0)
    low, high = (
        jnp.broadcast_to(mean[i * half : (i + 1) * half], (half, half)).T[:GROUP]
        for i in range(2)
    )
    out[3 * half :, :] = jnp.where(row == 0, low, jnp.where(row == 1, high, 0.0))


def moments(prior):
    size = prior.shape[0]
    return pl.pallas_call(
        moments_kernel,
        out_shape=(
            jax.ShapeDtypeStruct((3 * size // 2 + GROUP, size // 2), jnp.float32),
            jax.ShapeDtypeStruct(prior.shape, jnp.float32),
        ),
        compiler_params=pltpu.CompilerParams(vmem_limit_bytes=24 << 20),
        cost_estimate=pl.CostEstimate(
            flops=6 * size * size * prior.shape[1] * 2,
            bytes_accessed=4 * size * prior.shape[1],
            transcendentals=0,
        ),
    )(prior)


def merged(mine, other, count):
    half = mine.shape[1]
    delta = mine[3 * half :] - other[3 * half :]
    row = lax.broadcasted_iota(jnp.int32, delta.shape, 0)
    parts = [jnp.where(row == 0, jnp.broadcast_to(delta[i : i + 1], delta.shape), 0.0) for i in (0, 1)]
    out = []
    for n, (i, j) in enumerate(((0, 0), (1, 0), (1, 1))):
        place = slice(n * half, (n + 1) * half)
        outer = lax.dot_general(
            parts[i],
            parts[j],
            (((0,), (0,)), ((), ())),
            precision=finest,
            preferred_element_type=jnp.float32,
        )
        out.append(mine[place] + other[place] + outer * (count / 2))
    out.append((mine[3 * half :] + other[3 * half :]) / 2)
    return out


def merge_kernel(count, mine, other, out):
    half = mine.shape[1]
    parts = merged(mine[...], other[...], count)
    for n in range(3):
        out[n * half : (n + 1) * half, :] = parts[n]
    out[3 * half :, :] = parts[3]


def merge(mine, other, count):
    def body(*refs):
        merge_kernel(count, *refs)

    return pl.pallas_call(
        body,
        out_shape=jax.ShapeDtypeStruct(mine.shape, jnp.float32),
        compiler_params=pltpu.CompilerParams(vmem_limit_bytes=16 << 20),
    )(mine, other)


def inverse_kernel(members, states, reach, mine, other, var_row, off_col, off_row, out):
    half = LANES
    size = 2 * half
    tiles = 2
    parts = merged(mine[...], other[...], members // 2)
    square = ((parts[0], parts[1]), (parts[1].T, parts[2]))
    rows = lax.broadcasted_iota(jnp.int32, (half, half), 0)
    lanes = lax.broadcasted_iota(jnp.int32, (half, half), 1)
    for t in range(tiles):
        cols = slice(t * half, (t + 1) * half)
        for i in range(tiles):
            place = slice(i * half, (i + 1) * half)
            cov = cycle_taper(off_col[place], off_row[:, cols], states, reach) * (
                square[t][i] / (members - 1)
            )
            if i == t:
                cov = cov + jnp.where(rows == lanes, var_row[:, cols], 0.0)
            out[t, place, :] = cov
    row = lax.broadcasted_iota(jnp.int32, (STEP, half), 0)
    lane = lax.broadcasted_iota(jnp.int32, (STEP, half), 1)
    wide = lax.broadcasted_iota(jnp.int32, (size, half), 1)

    def over(x):
        return jnp.broadcast_to(x, (STEP, half))

    current = [out[q, 0:STEP, :] for q in range(tiles)]
    for at in range(0, size, STEP):
        t, base = divmod(at, half)
        inside = (lane >= base) & (lane < base + STEP)
        unit = (lane - base == row).astype(jnp.float32)
        columns = [over(current[t][:, base + j : base + j + 1]) for j in range(STEP)]
        pivots = [jnp.where(inside, unit, x) if q == t else x for q, x in enumerate(current)]
        last = at + STEP == size
        if not last:
            ahead = [out[q, at + STEP : at + 2 * STEP, :] for q in range(tiles)]
            factors = [over(ahead[t][:, base + j : base + j + 1]) for j in range(STEP)]
        for k in range(STEP):
            inv = 1.0 / over(columns[k][k : k + 1])
            factor = columns[k]
            on_row = row == k

            def eliminate(x):
                scaled = over(x[k : k + 1]) * inv
                return jnp.where(on_row, scaled, x - factor * scaled)

            for j in range(k + 1, STEP):
                columns[j] = eliminate(columns[j])
            pivots = [eliminate(x) for x in pivots]
        if not last:
            current = []
            for q in range(tiles):
                acc = jnp.where(inside, 0.0, ahead[q]) if q == t else ahead[q]
                for j in range(STEP):
                    acc = acc - factors[j] * over(pivots[q][j : j + 1])
                current.append(acc)
        panel = out[t, :, :][:, base : base + STEP]
        for q in range(tiles):
            old = out[q]
            if q == t:
                old = jnp.where((wide >= base) & (wide < base + STEP), 0.0, old)
            out[q] = old - jnp.dot(
                panel, pivots[q], precision=finest, preferred_element_type=jnp.float32
            )
        for q in range(tiles):
            out[q, at : at + STEP, :] = pivots[q]


def inverse_cov(mine, other, variance, places, members, states, reach):
    size = places.shape[0]

    def body(*refs):
        inverse_kernel(members, states, reach, *refs)

    tiled = pl.pallas_call(
        body,
        out_shape=jax.ShapeDtypeStruct((size // LANES, size, LANES), jnp.float32),
        compiler_params=pltpu.CompilerParams(vmem_limit_bytes=16 << 20),
        cost_estimate=pl.CostEstimate(flops=8 * 10**9, bytes_accessed=1 << 20, transcendentals=0),
    )(mine, other, variance[None, :], places[:, None], places[None, :])
    return jnp.concatenate([tiled[t] for t in range(size // LANES)], axis=1)


def local(ensemble, obs_values, obs_noise, obs_var, obs_offset, owner):
    rows, width = ensemble.shape
    members = width * lax.axis_size(ENS)
    states = rows * lax.axis_size(STATE)
    reach = states // 4
    here = lax.axis_index(STATE)
    positions = here * rows + jnp.arange(rows, dtype=jnp.int32)
    places = [owner[b] * rows + obs_offset[b] for b in range(NB)]

    def misfit(batch, prior):
        return (
            obs_values[batch][:, None]
            + jnp.sqrt(obs_var[batch])[:, None] * obs_noise[batch].astype(jnp.float32)
            - prior
        )

    def products(x, anom):
        return jnp.einsum("pm,sm->ps", anom, x, precision=close), jnp.sum(x, axis=1)

    def shifted(cross, total, shift):
        return pair_sum(cross + shift.reshape(-1, 1) * total[None, :])

    def gain_of(cross, spots, batch, inverse):
        gain = cycle_taper(spots[:, None], places[batch][None, :], states, reach) * (
            cross / (members - 1)
        )
        return jnp.dot(gain, inverse, precision=close)

    def own_gain(cross, batch, inverse):
        gain = cycle_taper(places[batch][:, None], positions[None, :], states, reach) * (
            cross / (members - 1)
        )
        return jnp.einsum("ps,pq->sq", gain, inverse, precision=close)

    def update(x, gain, values):
        return x + jnp.dot(gain, values, precision=close)

    def statistics(prior):
        stats, anom = moments(prior)
        own = stats[-GROUP:][:2]
        stats = merge(stats, swap(stats, "core"), width)
        return own, anom, stats

    def shift_of(own, stats, other):
        whole = ((stats[-GROUP:] + other[-GROUP:]) / 2)[:2]
        return (own - whole).reshape(1, 2 * own.shape[1])

    prior, second = spread_rows(ensemble, obs_offset, owner)
    prior, second = lax.optimization_barrier((prior, plane_copies(second)))
    later = plane_gather(second)
    own, anom, stats = statistics(prior)
    other = swap(stats, "zl")
    mine = products(ensemble, anom)
    shift = shift_of(own, stats, other)
    inverse = inverse_cov(stats, other, obs_var[0], places[0], members, states, reach)
    centered = anom + shift.reshape(-1, 1)
    values = misfit(0, prior)
    mine, centered, values, inverse = lax.optimization_barrier((mine, centered, values, inverse))
    theirs = pair_sum(jnp.einsum("sm,pm->sp", later, centered, precision=close))
    theirs, mine = lax.optimization_barrier((theirs, mine))
    theirs = whole_sum(theirs, swap(theirs, "zl"))
    kept = shifted(*mine, shift)
    moved = swap(kept, "zl")
    prior = update(later, gain_of(theirs, places[1], 0, inverse), values)
    gain = own_gain(whole_sum(kept, moved), 0, inverse)
    current = update(ensemble, gain, values)

    own, anom, stats = statistics(prior)
    other = swap(stats, "zl")
    cross = products(current, anom)
    kept = shifted(*cross, shift_of(own, stats, other))
    stats, kept = lax.optimization_barrier((stats, kept))
    moved = swap(kept, "zl")
    inverse = inverse_cov(stats, other, obs_var[1], places[1], members, states, reach)
    moved, inverse = lax.optimization_barrier((moved, inverse))
    gain = own_gain(whole_sum(kept, moved), 1, inverse)
    return update(current, gain, misfit(1, prior))


def solution(mesh):
    ens, state = mesh.devices.shape
    fine = Mesh(
        mesh.devices.reshape(2, ens // 2, 4, state // 16, 4), ("zl", "core", "y", "zh", "x")
    )
    in_specs = (P(STATE, ENS), P(), P(None, None, ENS), P(), P(), P())
    return jax.shard_map(
        local, mesh=fine, in_specs=in_specs, out_specs=P(STATE, ENS), check_vma=False
    )
```
